32 devices in a mesh: seq: 16 (over z, y, x), head: 2 (over core).
Axes of the slice: x: 2, y: 2, z: 4, core: 2. Of those that a mesh axis runs over, the one named last changes fastest.
Arguments:
- queries: bfloat16 [2048, 4096], P('seq', 'head'), may hold values from -6 to 6
- keys: bfloat16 [2048, 4096], P('seq', 'head'), may hold values from -6 to 6
- values: bfloat16 [2048, 4096], P('seq', 'head'), may hold values from -6 to 6
- level_index: int32 [2048, 8], P('seq'), may hold values from 0 to 15
- level_table: float32 [32, 16], P('head'), may hold values from 0.25 to 4
- out_weight: bfloat16 [4096, 4096], P('head', 'seq'), may hold values from -0.09375 to 0.09375
Outputs:
- output: bfloat16 [2048, 4096], P('seq', 'head')
The draws below stay inside these ranges and needn't reach their ends.
All inputs are finite; a program needn't handle non-finite values.
Results may differ from the reference program's by a relative error of at most 0.0057.
Values may be sent and summed in bfloat16 or wider, within the bound.
No kernel may reach another device: no remote copies, remote signals or barrier semaphores. Data moves between devices by JAX's collectives and lax.ppermute only.
A program may use at most 64 MiB of HBM per device.

```python
import math
import jax
import jax.numpy as jnp
from jax import lax

DH = 128
HEADS = 32
D = 4096
VALS = 16
LEVELS = 8
TOK_DEV = 128
TOKENS = 2048
N_SEQ = 16


def place_ends(values, own_key, smallest, largest):
    index_at = [jax.random.randint(jax.random.fold_in(own_key, axis), (), 0, length) for axis, length in enumerate(values.shape)]
    longest = values.shape.index(max(values.shape))
    next_to = index_at[:longest] + [(index_at[longest] + 1) % values.shape[longest]] + index_at[longest + 1:]
    return values.at[tuple(index_at)].set(smallest).at[tuple(next_to)].set(largest)


def block_levels(own_key, shape, cuts, smallest, high):
    def one(axis_at, blocks):
        heights = jax.random.uniform(jax.random.fold_in(jax.random.fold_in(own_key, 6), axis_at), (blocks,), jnp.float32, smallest / len(cuts), high / len(cuts))
        return jnp.repeat(jnp.exp(heights), shape[axis_at] // blocks).reshape((-1,) + (1,) * (len(shape) - axis_at - 1))

    loudness = one(*cuts[0])
    for cut in cuts[1:]:
        loudness = loudness * one(*cut)
    return loudness


def centred(own_key, extent, spread, reach, split=(), held_as=jnp.bfloat16):
    array = jax.random.normal(own_key, extent, jnp.float32) * spread
    if len(split) > 0:
        array = block_levels(own_key, extent, split, -0.22, 0.18) * array
    return jnp.clip(array, min=-reach, max=reach).astype(held_as)


def setup_inputs(seed: int = 0) -> dict:
    arg_keys = jax.random.split(jax.random.key(seed), 7)
    return {
        "queries": centred(arg_keys[0], (TOKENS, HEADS * DH), 1.0, 6.0, ((0, 16), (1, 2))),
        "keys": centred(arg_keys[1], (TOKENS, HEADS * DH), 1.0, 6.0, ((0, 16), (1, 2))),
        "values": centred(arg_keys[2], (TOKENS, HEADS * DH), 1.0, 6.0, ((0, 16), (1, 2))),
        "level_index": place_ends(jax.random.randint(arg_keys[3], (TOKENS, LEVELS), 0, VALS), jax.random.fold_in(arg_keys[3], 1), 0, VALS - 1).astype(jnp.int32),
        "level_table": jnp.clip(jnp.exp(math.log(4.0) - 2.7725887 * jax.random.uniform(arg_keys[4], (HEADS, VALS), jnp.float32) ** block_levels(arg_keys[4], (HEADS, VALS), ((0, 2),), -0.2, 0.2)), 0.25, 4.0),
        "out_weight": centred(arg_keys[5], (HEADS * DH, D), (HEADS * DH) ** -0.5, 0.09375, ((0, 2), (1, 16))),
    }


def stretch_work(items):
    query_rows, key_rows, value_rows, first_weight = items
    qf = query_rows.astype(jnp.float32)
    kf = key_rows.astype(jnp.float32)
    vf = value_rows.astype(jnp.float32)
    state = jnp.einsum('tha,thb->hab', kf, vf)
    scores = jnp.einsum('tha,sha->hts', qf, kf)
    factor = jnp.transpose(first_weight) * (1.0 / math.sqrt(DH) / math.sqrt(TOK_DEV))
    causal = jnp.arange(TOK_DEV)[:, None] >= jnp.arange(TOK_DEV)[None, :]
    weights = jnp.where(causal[None], scores * factor[:, :, None], 0.0).astype(jnp.bfloat16)
    mixed = jnp.einsum('hts,shb->thb', weights.astype(jnp.float32), vf)
    return (state, mixed)

def reference(queries, keys, values, level_index, level_table, out_weight):
    query_heads = queries.reshape(N_SEQ, TOK_DEV, HEADS, DH)
    key_heads = keys.reshape(N_SEQ, TOK_DEV, HEADS, DH)
    value_heads = values.reshape(N_SEQ, TOK_DEV, HEADS, DH)
    level_weight = jnp.transpose(level_table[:, level_index], (1, 2, 0)).reshape(N_SEQ, TOK_DEV, LEVELS, HEADS)
    states, mixed = lax.map(stretch_work, (query_heads, key_heads, value_heads, level_weight[:, :, 0, :]))
    stretch_ids = jnp.arange(N_SEQ, dtype=jnp.int32)
    block = states
    for level in range(N_SEQ.bit_length() - 1):
        span = 2 ** level
        partner = block[stretch_ids ^ span]
        upper_half = stretch_ids >> level & 1 == 1
        level_state = jnp.where(upper_half[:, None, None, None], partner, 0.0).astype(jnp.bfloat16)
        reads = jnp.einsum('ntha,nhab->nthb', query_heads.astype(jnp.float32), level_state.astype(jnp.float32))
        scale = level_weight[:, :, level + 1, :] * (1.0 / math.sqrt(DH) / math.sqrt(TOK_DEV * span))
        mixed = mixed + reads * scale[:, :, :, None]
        block = block + partner
    square = lax.optimization_barrier(jnp.mean(mixed * mixed, axis=-1, keepdims=True))
    normed = (mixed * lax.rsqrt(square + 1e-06)).astype(jnp.bfloat16).reshape(TOKENS, HEADS * DH)
    return jnp.dot(normed, out_weight, preferred_element_type=jnp.float32).astype(jnp.bfloat16)
```

```python
import math

import jax
import jax.numpy as jnp
from jax import lax
from jax.sharding import PartitionSpec as P

DH = 128
VALS = 16


def swap(value, axis, mask):
    pairs = [(source, source ^ mask) for source in range(lax.axis_size(axis))]
    return lax.ppermute(value, axis, pairs)


def lift(value, axis, mask):
    pairs = [(source, source ^ mask) for source in range(lax.axis_size(axis)) if not source & mask]
    return lax.ppermute(value, axis, pairs)


def masks_of(bits):
    out = [0]
    for bit in bits:
        out = out + [mask | 1 << bit for mask in out]
    return out


def spread(own, axis, bits):
    pieces = {0: own}
    for bit in bits:
        for mask in list(pieces):
            pieces[mask | 1 << bit] = swap(pieces[mask], axis, 1 << bit)
    return pieces


def absolute(pieces, bits, position):
    for bit in bits:
        flag = position >> bit & 1 == 1
        ordered = {}
        for mask, piece in pieces.items():
            ordered[mask] = jnp.where(flag, pieces[mask ^ 1 << bit], piece)
        pieces = ordered
    return pieces


def level_states(state, position, depth):
    heads = state.shape[0]
    half = heads // 2
    own = state.astype(jnp.bfloat16)
    set_at = lambda level: position >> level & 1 == 1
    near = swap(own, "seq", 1)
    side = swap(own, "seq", 2)
    corner = (swap(side[:half], "seq", 1), swap(near[half:], "seq", 2))
    read = [[], []]
    for part in range(2):
        rows = slice(part * half, (part + 1) * half)
        pair = side[rows].astype(jnp.float32) + corner[part].astype(jnp.float32)
        block = state[rows] + near[rows].astype(jnp.float32) + pair
        read[part].append(jnp.where(set_at(0), near[rows], jnp.bfloat16(0)))
        read[part].append(jnp.where(set_at(1), pair, 0.0).astype(jnp.bfloat16))
        for level in range(2, depth):
            sent = block.astype(jnp.bfloat16)
            if level == depth - 1:
                read[part].append(lift(sent, "seq", 1 << level))
            else:
                other = swap(sent, "seq", 1 << level)
                read[part].append(jnp.where(set_at(level), other, jnp.bfloat16(0)))
                block = block + other.astype(jnp.float32)
    return read


def shards(queries, keys, values, level_index, level_table, out_weight):
    rows = queries.shape[0]
    heads_here = level_table.shape[0]
    position = lax.axis_index("seq")
    core = lax.axis_index("head")
    depth = lax.axis_size("seq").bit_length() - 1
    top = depth - 1
    token_bits = [1, 2] if depth < 6 else [1, 2, 3]
    column_bits = [bit for bit in range(depth - 1) if bit not in token_bits]

    key_heads = keys.reshape(rows, heads_here, DH)
    value_heads = values.reshape(rows, heads_here, DH)
    query_heads = queries.reshape(rows, heads_here, DH)
    state = jnp.einsum("tha,thb->hab", key_heads, value_heads, preferred_element_type=jnp.float32)
    read = level_states(state, position, depth)

    weights_of = spread(out_weight, "seq", [top] + column_bits)

    onehot = (level_index[:, :, None] == jnp.arange(VALS, dtype=jnp.int32)[None, None, :]).astype(
        jnp.float32
    )
    level_weight = jnp.einsum("tlv,hv->tlh", onehot, level_table, precision=lax.Precision.HIGHEST)
    inv_root = 1.0 / math.sqrt(DH)
    scores = jnp.einsum("tha,sha->hts", query_heads, key_heads, preferred_element_type=jnp.float32)
    factor = jnp.transpose(level_weight[:, 0, :]) * (inv_root / math.sqrt(rows))
    causal = jnp.arange(rows)[:, None] >= jnp.arange(rows)[None, :]
    weights = jnp.where(causal[None], scores * factor[:, :, None], 0.0).astype(jnp.bfloat16)
    mixed = jnp.einsum("hts,shb->thb", weights, value_heads, preferred_element_type=jnp.float32)

    half = heads_here // 2
    normed = []
    for part in range(2):
        cut = slice(part * half, (part + 1) * half)
        total = mixed[:, cut]
        for level in range(depth):
            reads = jnp.einsum(
                "tha,hab->thb", query_heads[:, cut], read[part][level], preferred_element_type=jnp.float32
            )
            scale = level_weight[:, level + 1, cut] * (inv_root / math.sqrt(rows * 2**level))
            total = total + reads * scale[:, :, None]
        square = jnp.mean(total * total, axis=-1, keepdims=True)
        normed.append((total * lax.rsqrt(square + 1e-06)).astype(jnp.bfloat16).reshape(rows, half * DH))
    normed = jnp.concatenate(normed, axis=1)

    tokens_of = spread(normed, "seq", token_bits)
    token_masks = sorted(tokens_of)
    tokens = jnp.concatenate([tokens_of[mask] for mask in token_masks], axis=0)

    mine = (position >> top & 1) == core
    sums = {}
    for mask in masks_of(column_bits):
        first = jnp.dot(tokens, weights_of[mask], preferred_element_type=jnp.float32)
        second = jnp.dot(tokens, weights_of[mask | 1 << top], preferred_element_type=jnp.float32)
        keep = jnp.where(mine, first, second)
        give = jnp.where(mine, second, first)
        sums[mask] = (keep, give.astype(jnp.bfloat16))
    for mask, (keep, give) in list(sums.items()):
        sums[mask] = (keep + swap(give, "head", 1).astype(jnp.float32)).astype(jnp.bfloat16)
    sums = absolute(sums, column_bits, position)
    column_masks = sorted(sums)
    summed = jnp.concatenate([sums[mask] for mask in column_masks], axis=1)
    landed = {}
    for at, mask in enumerate(token_masks):
        piece = summed[at * rows : (at + 1) * rows]
        landed[mask] = swap(piece, "seq", mask) if mask else piece
    landed = absolute(landed, token_bits, position)
    width = out_weight.shape[1]
    columns = {}
    for mask, piece in landed.items():
        for at, column_mask in enumerate(column_masks):
            columns[mask | column_mask] = piece[:, at * width : (at + 1) * width]
    return jnp.concatenate([columns[mask] for mask in sorted(columns)], axis=1)


def solution(mesh):
    placed = (
        P("seq", "head"),
        P("seq", "head"),
        P("seq", "head"),
        P("seq", None),
        P("head", None),
        P("head", "seq"),
    )
    return jax.shard_map(
        shards, mesh=mesh, in_specs=placed, out_specs=P("seq", "head"), check_vma=False
    )
```

```python
import math

import jax
import jax.numpy as jnp
from jax import lax
from jax.sharding import PartitionSpec as P

DH = 128
VALS = 16


def swap(value, mask):
    pairs = [(source, source ^ mask) for source in range(lax.axis_size("seq"))]
    return lax.ppermute(value, "seq", pairs)


def lift(value, mask):
    pairs = [(source, source ^ mask) for source in range(lax.axis_size("seq")) if not source & mask]
    return lax.ppermute(value, "seq", pairs)


def swap_cores(value):
    return lax.ppermute(value, "head", [(0, 1), (1, 0)])


def send_home(value, mask, top):
    pairs = []
    for source in range(lax.axis_size("seq")):
        for core in range(2):
            target = source ^ mask ^ (core << top)
            pairs.append((source * 2 + core, target * 2 + (source >> top & 1)))
    return lax.ppermute(value, ("seq", "head"), pairs)


def masks_of(bits):
    out = [0]
    for bit in bits:
        out = out + [mask | 1 << bit for mask in out]
    return out


def spread(own, bits):
    pieces = {0: own}
    for bit in bits:
        for mask in list(pieces):
            pieces[mask | 1 << bit] = swap(pieces[mask], 1 << bit)
    return pieces


def absolute(pieces, bits, position):
    for bit in bits:
        flag = position >> bit & 1 == 1
        pieces = {mask: jnp.where(flag, pieces[mask ^ 1 << bit], piece) for mask, piece in pieces.items()}
    return pieces


def groups(depth):
    low_token_bits = [1] if depth < 6 else [1, 2]
    column_bits = [bit for bit in range(depth - 1) if bit not in low_token_bits][::-1]
    return low_token_bits, column_bits


def level_states(state, position, depth):
    top = depth - 1
    wide = lambda value: value.astype(jnp.float32)
    set_at = lambda level: position >> level & 1 == 1
    none = jnp.bfloat16(0)
    own = [part.astype(jnp.bfloat16) for part in state]
    near, side, corner = [None, None], [None, None], [None, None]
    near[0] = swap(own[0], 1)
    side[0] = swap(own[1], 2)
    corner[0] = swap(side[0], 1)
    side[1] = swap(own[0], 2)
    near[1] = swap(own[1], 1)
    corner[1] = swap(near[0], 2)
    read = []
    for part in range(2):
        pair = wide(side[part]) + wide(corner[part])
        block = state[part] + wide(near[part]) + pair
        mine = [
            jnp.where(set_at(0), near[part], none),
            jnp.where(set_at(1), pair, 0.0).astype(jnp.bfloat16),
        ]
        for level in range(2, top):
            if part == 1 and level == top - 1:
                mine.append(lift(block.astype(jnp.bfloat16), 1 << level))
            else:
                other = swap(block.astype(jnp.bfloat16), 1 << level)
                mine.append(jnp.where(set_at(level), other, none))
                block = block + wide(other)
        if part == 0:
            last = lift(block.astype(jnp.bfloat16), 1 << top)
            mine.append(last)
        else:
            mine.append(swap(last, 2))
        read.append(mine)
    return read


def shards(queries, keys, values, level_index, level_table, out_weight):
    rows = queries.shape[0]
    heads_here = level_table.shape[0]
    half = heads_here // 2
    position = lax.axis_index("seq")
    core = lax.axis_index("head")
    depth = lax.axis_size("seq").bit_length() - 1
    top = depth - 1
    low_token_bits, column_bits = groups(depth)

    flip = position >> 1 & 1
    flipped = flip == 1
    starts = [flip * half, (1 - flip) * half]

    def halves(value):
        return [
            lax.dynamic_slice_in_dim(value, start * DH, half * DH, 1).reshape(rows, half, DH)
            for start in starts
        ]

    query_heads, key_heads, value_heads = halves(queries), halves(keys), halves(values)
    state = [
        jnp.einsum("tha,thb->hab", key, value, preferred_element_type=jnp.float32)
        for key, value in zip(key_heads, value_heads)
    ]
    weights_of = spread(out_weight, column_bits)
    read = level_states(state, position, depth)

    onehot = (level_index[:, :, None] == jnp.arange(VALS, dtype=jnp.int32)[None, None, :]).astype(
        jnp.float32
    )
    level_weight = jnp.einsum("tlv,hv->tlh", onehot, level_table, precision=lax.Precision.HIGHEST)
    inv_root = 1.0 / math.sqrt(DH)
    causal = jnp.arange(rows)[:, None] >= jnp.arange(rows)[None, :]
    normed = []
    for part in range(2):
        lam = lax.dynamic_slice_in_dim(level_weight, starts[part], half, 2)
        scores = jnp.einsum(
            "tha,sha->hts", query_heads[part], key_heads[part], preferred_element_type=jnp.float32
        )
        factor = jnp.transpose(lam[:, 0, :]) * (inv_root / math.sqrt(rows))
        weights = jnp.where(causal[None], scores * factor[:, :, None], 0.0).astype(jnp.bfloat16)
        total = jnp.einsum("hts,shb->thb", weights, value_heads[part], preferred_element_type=jnp.float32)
        for level in range(depth):
            reads = jnp.einsum("tha,hab->thb", query_heads[part], read[part][level], preferred_element_type=jnp.float32)
            scale = lam[:, level + 1, :] * (inv_root / math.sqrt(rows * 2**level))
            total = total + reads * scale[:, :, None]
        square = jnp.mean(total * total, axis=-1, keepdims=True)
        normed.append((total * lax.rsqrt(square + 1e-06)).astype(jnp.bfloat16).reshape(rows, half * DH))

    pieces = {0: tuple(normed)}
    for bit in [top] + low_token_bits:
        for mask in list(pieces):
            new = mask | 1 << bit
            got = [swap(pieces[mask][part], 1 << bit) for part in range(2)]
            pieces[new] = tuple(got[::-1] if bit == 1 else got)
    token_masks = masks_of(low_token_bits)
    token_masks = token_masks + [mask | 1 << top for mask in token_masks]
    tokens = jnp.concatenate(
        [
            jnp.where(
                flipped,
                jnp.concatenate(pieces[mask][::-1], axis=1),
                jnp.concatenate(pieces[mask], axis=1),
            )
            for mask in token_masks
        ],
        axis=0,
    )
    column_masks = sorted(weights_of)
    kept = tokens.shape[0] // 2
    first_core = core == 0
    sums = {}
    for mask in column_masks:
        part = jnp.dot(tokens, weights_of[mask], preferred_element_type=jnp.float32)
        keep = jnp.where(first_core, part[:kept], part[kept:])
        give = jnp.where(first_core, part[kept:], part[:kept]).astype(jnp.bfloat16)
        sums[mask] = (keep + swap_cores(give).astype(jnp.float32)).astype(jnp.bfloat16)
    sums = absolute(sums, column_bits, position)
    summed = jnp.concatenate([sums[mask] for mask in column_masks], axis=1)
    landed = {}
    for at, mask in enumerate(masks_of(low_token_bits)):
        landed[mask] = send_home(summed[at * rows : (at + 1) * rows], mask, top)
    landed = absolute(landed, low_token_bits, position)
    width = out_weight.shape[1]
    columns = {}
    for mask, piece in landed.items():
        for at, column_mask in enumerate(column_masks):
            columns[mask | column_mask] = piece[:, at * width : (at + 1) * width]
    return jnp.concatenate([columns[mask] for mask in sorted(columns)], axis=1)


def solution(mesh):
    placed = (
        P("seq", "head"),
        P("seq", "head"),
        P("seq", "head"),
        P("seq", None),
        P("head", None),
        P("head", "seq"),
    )
    return jax.shard_map(
        shards, mesh=mesh, in_specs=placed, out_specs=P("seq", "head"), check_vma=False
    )
```

```python
import math

import jax
import jax.numpy as jnp
from jax import lax
from jax.sharding import PartitionSpec as P

DH = 128
VALS = 16


def swap(value, mask):
    pairs = [(source, source ^ mask) for source in range(lax.axis_size("seq"))]
    return lax.ppermute(value, "seq", pairs)


def lift(value, clear, need, mask):
    pairs = [
        (source, source ^ mask)
        for source in range(lax.axis_size("seq"))
        if not source & clear and source & need == need
    ]
    return lax.ppermute(value, "seq", pairs)


def swap_cores(value):
    return lax.ppermute(value, "head", [(0, 1), (1, 0)])


def masks_of(bits):
    out = [0]
    for bit in bits:
        out = out + [mask | 1 << bit for mask in out]
    return out


def absolute(pieces, bits, position):
    for bit in bits:
        flag = position >> bit & 1 == 1
        pieces = {mask: jnp.where(flag, pieces[mask ^ 1 << bit], piece) for mask, piece in pieces.items()}
    return pieces


def groups(depth):
    top = depth - 1
    token_bits = [1, top - 1] if depth < 6 else [1, 2, top - 1]
    column_bits = [bit for bit in range(top) if bit not in token_bits][::-1]
    return token_bits, column_bits


def level_states(state, position, depth):
    top = depth - 1
    wide = lambda value: value.astype(jnp.float32)
    set_at = lambda level: position >> level & 1 == 1
    none = jnp.bfloat16(0)
    own = [part.astype(jnp.bfloat16) for part in state]
    near, side, corner = [None, None], [None, None], [None, None]
    side[0] = swap(own[1], 2)
    near[0] = swap(own[0], 1)
    side[1] = swap(own[0], 2)
    corner[0] = swap(side[0], 1)
    near[1] = swap(own[1], 1)
    corner[1] = swap(near[0], 2)
    read = []
    for part in range(2):
        pair = wide(side[part]) + wide(corner[part])
        block = state[part] + wide(near[part]) + pair
        mine = [
            jnp.where(set_at(0), near[part], none),
            jnp.where(set_at(1), pair, 0.0).astype(jnp.bfloat16),
        ]
        for level in range(2, top):
            sent = block.astype(jnp.bfloat16)
            if level == top - 1 and part == 0:
                other = lift(sent, 1 << level | 1 << top, 0, 1 << level)
                upper = lift(sent, 1 << level, 1 << top, 1 << level)
                mine.append(other + upper)
            elif level == top - 1:
                other = lift(sent, 1 << level, 0, 1 << level)
                mine.append(other)
            else:
                other = swap(sent, 1 << level)
                mine.append(jnp.where(set_at(level), other, none))
            block = block + wide(other)
        if part == 0:
            sent = block.astype(jnp.bfloat16)
            below = 1 << top - 1
            far = lift(sent, 1 << top, below, 1 << top)
            close = lift(sent, 1 << top, below, 1 << top | below)
            last = far + close
            mine.append(last)
        else:
            mine.append(swap(last, 2))
        read.append(mine)
    return read


def shards(queries, keys, values, level_index, level_table, out_weight):
    rows = queries.shape[0]
    heads_here = level_table.shape[0]
    half = heads_here // 2
    position = lax.axis_index("seq")
    core = lax.axis_index("head")
    depth = lax.axis_size("seq").bit_length() - 1
    top = depth - 1
    token_bits, column_bits = groups(depth)

    flip = position >> 1 & 1
    starts = [flip * half, (1 - flip) * half]

    def halves(value):
        return [
            lax.dynamic_slice_in_dim(value, start * DH, half * DH, 1).reshape(rows, half, DH)
            for start in starts
        ]

    query_heads, key_heads, value_heads = halves(queries), halves(keys), halves(values)
    state = [
        jnp.einsum("tha,thb->hab", key, value, preferred_element_type=jnp.float32)
        for key, value in zip(key_heads, value_heads)
    ]
    ordered = jnp.concatenate(
        [lax.dynamic_slice_in_dim(out_weight, start * DH, half * DH, 0) for start in starts], axis=0
    )
    split = ordered.shape[0] * 5 // 8
    parts = (ordered[:split], ordered[split:])
    weights_of = {1 << top: tuple(swap(part, 1 << top) for part in parts)}
    weights_of[0] = parts
    for bit in column_bits:
        for mask in list(weights_of):
            new = mask | 1 << bit
            weights_of[new] = tuple(swap(part, 1 << bit) for part in weights_of[mask])
    read = level_states(state, position, depth)

    onehot = (level_index[:, :, None] == jnp.arange(VALS, dtype=jnp.int32)[None, None, :]).astype(
        jnp.float32
    )
    level_weight = jnp.einsum("tlv,hv->tlh", onehot, level_table, precision=lax.Precision.HIGHEST)
    inv_root = 1.0 / math.sqrt(DH)
    causal = jnp.arange(rows)[:, None] >= jnp.arange(rows)[None, :]
    normed = []
    for part in range(2):
        lam = lax.dynamic_slice_in_dim(level_weight, starts[part], half, 2)
        scores = jnp.einsum(
            "tha,sha->hts", query_heads[part], key_heads[part], preferred_element_type=jnp.float32
        )
        factor = jnp.transpose(lam[:, 0, :]) * (inv_root / math.sqrt(rows))
        weights = jnp.where(causal[None], scores * factor[:, :, None], 0.0).astype(jnp.bfloat16)
        total = jnp.einsum("hts,shb->thb", weights, value_heads[part], preferred_element_type=jnp.float32)
        for level in range(depth):
            reads = jnp.einsum("tha,hab->thb", query_heads[part], read[part][level], preferred_element_type=jnp.float32)
            scale = lam[:, level + 1, :] * (inv_root / math.sqrt(rows * 2**level))
            total = total + reads * scale[:, :, None]
        square = jnp.mean(total * total, axis=-1, keepdims=True)
        normed.append((total * lax.rsqrt(square + 1e-06)).astype(jnp.bfloat16).reshape(rows, half * DH))

    pieces = {0: tuple(normed)}
    for mask in masks_of(token_bits)[1:]:
        bits = [bit for bit in token_bits if mask >> bit & 1]
        got = []
        for part in range(2):
            bit = bits[0] if part else bits[-1]
            source = 1 - part if bit == 1 else part
            got.append(swap(pieces[mask ^ 1 << bit][source], 1 << bit))
        pieces[mask] = tuple(got)
    token_masks = sorted(pieces)
    tokens = jnp.concatenate(
        [jnp.concatenate([pieces[mask][part] for part in range(2)], axis=1) for mask in token_masks],
        axis=0,
    )
    mine = (position >> top & 1) == core

    def product(mask):
        first, second = weights_of[mask]
        return jnp.dot(tokens[:, :split], first, preferred_element_type=jnp.float32) + jnp.dot(
            tokens[:, split:], second, preferred_element_type=jnp.float32
        )

    landed = {}
    for mask in masks_of(column_bits):
        near_half, far_half = lax.optimization_barrier((product(mask), product(mask | 1 << top)))
        keep = jnp.where(mine, near_half, far_half)
        give = jnp.where(mine, far_half, near_half).astype(jnp.bfloat16)
        summed = (keep + swap_cores(give).astype(jnp.float32)).astype(jnp.bfloat16)
        for at, token_mask in enumerate(token_masks):
            piece = summed[at * rows : (at + 1) * rows]
            whole = mask | token_mask
            landed[whole] = swap(piece, token_mask) if token_mask else piece
    landed = absolute(landed, token_bits + column_bits, position)
    return jnp.concatenate([landed[mask] for mask in sorted(landed)], axis=1)


def solution(mesh):
    placed = (
        P("seq", "head"),
        P("seq", "head"),
        P("seq", "head"),
        P("seq", None),
        P("head", None),
        P("head", "seq"),
    )
    return jax.shard_map(
        shards, mesh=mesh, in_specs=placed, out_specs=P("seq", "head"), check_vma=False
    )
```

```python
import math

import jax
import jax.numpy as jnp
from jax import lax
from jax.experimental import pallas as pl
from jax.experimental.pallas import tpu as pltpu
from jax.sharding import PartitionSpec as P

DH = 128


def swap(value, mask):
    pairs = [(source, source ^ mask) for source in range(lax.axis_size("seq"))]
    return lax.ppermute(value, "seq", pairs)


def lift(value, clear, need, mask):
    pairs = [
        (source, source ^ mask)
        for source in range(lax.axis_size("seq"))
        if not source & clear and source & need == need
    ]
    return lax.ppermute(value, "seq", pairs)


def swap_some(value, mask, half, upper):
    pairs = [
        (source, source ^ mask)
        for source in range(lax.axis_size("seq"))
        if (source & half != 0) == bool(upper)
    ]
    return lax.ppermute(value, "seq", pairs)


def swap_cores(value):
    return lax.ppermute(value, "head", [(0, 1), (1, 0)])


def masks_of(bits):
    out = [0]
    for bit in bits:
        out = out + [mask | 1 << bit for mask in out]
    return out


def groups(depth):
    top = depth - 1
    token_bits = [1, top - 1] if depth < 6 else [1, 2, top - 1]
    column_bits = [bit for bit in range(top) if bit not in token_bits][::-1]
    return token_bits, column_bits


HERE = pl.BlockSpec(memory_space=pltpu.VMEM)
FLAT = pl.BlockSpec(memory_space=pltpu.SMEM)
SMALL = pltpu.CompilerParams(vmem_limit_bytes=8 << 20)
F32, BF16 = jnp.float32, jnp.bfloat16


def local(kernel, scalars, operands, results):
    placed = [pltpu.with_memory_space_constraint(operand, pltpu.VMEM) for operand in operands]
    return pl.pallas_call(
        kernel,
        out_shape=tuple(pltpu.VMEM(shape, dtype) for shape, dtype in results),
        in_specs=[FLAT] * len(scalars) + [HERE] * len(operands),
        out_specs=tuple(HERE for _ in results),
        compiler_params=SMALL,
    )(*scalars, *placed)


def head_slice(start, head):
    return pl.ds(pl.multiple_of((start + head) * DH, DH), DH)


def states(flip, keys, values, half):
    rows, depth = keys.shape[0], half * DH

    def kernel(flip_ref, key_hbm, value_hbm, sum1_ref, own1_ref, sum0_ref, own0_ref, key_ref, value_ref, sems):
        copies = {}
        for part in (1, 0):
            start = pl.multiple_of(jnp.where(flip_ref[0] == part, 0, depth), depth)
            for at, (source, target) in enumerate(((key_hbm, key_ref), (value_hbm, value_ref))):
                copies[part, at] = pltpu.make_async_copy(
                    source.at[:, pl.ds(start, depth)], target.at[part], sems.at[part, at]
                )
                copies[part, at].start()
        for part, sum_ref, own_ref in ((1, sum1_ref, own1_ref), (0, sum0_ref, own0_ref)):
            copies[part, 0].wait()
            copies[part, 1].wait()
            for head in range(half):
                cut = slice(head * DH, (head + 1) * DH)
                state = lax.dot_general(
                    key_ref[part, :, cut],
                    value_ref[part, :, cut],
                    (((0,), (0,)), ((), ())),
                    preferred_element_type=F32,
                )
                sum_ref[head] = state
                own_ref[head] = state.astype(BF16)

    shape = (half, DH, DH)
    anywhere = pl.BlockSpec(memory_space=pltpu.HBM)
    made = pl.pallas_call(
        kernel,
        out_shape=(jax.ShapeDtypeStruct(shape, F32), pltpu.VMEM(shape, BF16)) * 2,
        in_specs=[FLAT, anywhere, anywhere],
        out_specs=(HERE,) * 4,
        scratch_shapes=[
            pltpu.VMEM((2, rows, depth), BF16),
            pltpu.VMEM((2, rows, depth), BF16),
            pltpu.SemaphoreType.DMA((2, 2)),
        ],
        compiler_params=SMALL,
        name="state",
    )(flip, *(pltpu.with_memory_space_constraint(operand, pltpu.HBM) for operand in (keys, values)))
    return [made[2:], made[:2]]


def merge(down, up):
    def kernel(down_ref, up_ref, out_ref):
        out_ref[...] = down_ref[...] + up_ref[...]

    return local(kernel, [], [down, up], [(down.shape, BF16)])[0]


def order_rows(flip, weight, split):
    depth, width = weight.shape
    half = depth // 2
    sizes = (split, depth - split)

    def kernel(flip_ref, weight_ref, *refs):
        out_refs, sems = refs[:2], refs[2]
        copies = []
        for out, (low, size) in enumerate(((0, split), (split, depth - split))):
            for which in range(2):
                begin, end = max(low, which * half), min(low + size, (which + 1) * half)
                if begin < end:
                    start = pl.multiple_of(jnp.where(flip_ref[0] == which, 0, half), half)
                    copies.append(
                        pltpu.make_async_copy(
                            weight_ref.at[pl.ds(start + begin - which * half, end - begin)],
                            out_refs[out].at[pl.ds(begin - low, end - begin)],
                            sems.at[len(copies)],
                        )
                    )
        for copy in copies:
            copy.start()
        for copy in copies:
            copy.wait()

    return pl.pallas_call(
        kernel,
        out_shape=tuple(pltpu.VMEM((size, width), weight.dtype) for size in sizes),
        in_specs=[FLAT, pl.BlockSpec(memory_space=pltpu.HBM)],
        out_specs=(HERE, HERE),
        scratch_shapes=[pltpu.SemaphoreType.DMA((4,))],
        compiler_params=SMALL,
        name="order",
    )(flip, pltpu.with_memory_space_constraint(weight, pltpu.HBM))


def level_scales(flip, position, level_index, level_table, roots, flags, half):
    rows, values = level_index.shape[0], level_table.shape[1]

    def kernel(flip_ref, position_ref, index_ref, table_ref, *out_refs):
        for part, out_ref in enumerate(out_refs):
            start = pl.multiple_of(jnp.where(flip_ref[0] == part, 0, half), half)
            table = table_ref[pl.ds(start, half), :]
            for level, root in enumerate(roots):
                chosen = index_ref[:, level : level + 1] == lax.broadcasted_iota(
                    jnp.int32, (rows, values), 1
                )
                lam = lax.dot_general(
                    chosen.astype(F32),
                    table,
                    (((1,), (1,)), ((), ())),
                    precision=lax.Precision.HIGHEST,
                    preferred_element_type=F32,
                )
                scale = lam * root
                if flags[level] is not None:
                    scale = jnp.where(position_ref[0] >> flags[level] & 1 == 1, scale, 0.0)
                out_ref[level] = scale

    shape = (len(roots), rows, half)
    return local(kernel, [flip, position], [level_index, level_table], [(shape, F32), (shape, F32)])


def block_sum(state, near, side, corner):
    def kernel(state_ref, near_ref, side_ref, corner_ref, sent_ref, block_ref):
        for head in range(state.shape[0]):
            pair = side_ref[head].astype(F32) + corner_ref[head].astype(F32)
            block = state_ref[head] + near_ref[head].astype(F32) + pair
            sent_ref[head] = block.astype(BF16)
            block_ref[head] = block

    results = [(state.shape, BF16), (state.shape, F32)]
    return local(kernel, [], [state, near, side, corner], results)


def add_block(block, other, wide):
    def kernel(block_ref, other_ref, *out_refs):
        for head in range(block.shape[0]):
            total = block_ref[head].astype(F32) + other_ref[head].astype(F32)
            for out_ref in out_refs:
                out_ref[head] = total.astype(out_ref.dtype)

    results = [(block.shape, BF16)] + [(block.shape, F32)] * wide
    return local(kernel, [], [block, other], results)


def first_reads(flip, queries, keys, values, scales, levels, half, part):
    rows = queries.shape[0]

    def kernel(flip_ref, query_ref, key_ref, value_ref, scale_ref, *refs):
        level_refs, total_ref = refs[:-1], refs[-1]
        start = jnp.where(flip_ref[0] == part, 0, half)
        causal = lax.broadcasted_iota(jnp.int32, (rows, rows), 0) >= lax.broadcasted_iota(
            jnp.int32, (rows, rows), 1
        )
        for head in range(half):
            cut = head_slice(start, head)
            query = query_ref[:, cut]
            scores = lax.dot_general(
                query, key_ref[:, cut], (((1,), (1,)), ((), ())), preferred_element_type=F32
            )
            weights = jnp.where(causal, scores * scale_ref[0, :, head : head + 1], 0.0).astype(BF16)
            total = jnp.dot(weights, value_ref[:, cut], preferred_element_type=F32)
            pair = (level_refs[1][head].astype(F32) + level_refs[2][head].astype(F32)).astype(BF16)
            found = [level_refs[0][head], pair] + [level_ref[head] for level_ref in level_refs[3:]]
            for at, level in enumerate(found):
                reads = jnp.dot(query, level, preferred_element_type=F32)
                total = total + reads * scale_ref[at + 1, :, head : head + 1]
            total_ref[:, head * DH : (head + 1) * DH] = total

    return local(kernel, [flip], [queries, keys, values, scales, *levels], [((rows, half * DH), F32)])[0]


def last_reads(flip, queries, scales, total, levels, half, part):
    rows = queries.shape[0]
    index = [at for _, at in levels]

    def kernel(flip_ref, query_ref, scale_ref, total_ref, *refs):
        level_refs, normed_ref = refs[:-1], refs[-1]
        start = jnp.where(flip_ref[0] == part, 0, half)
        for head in range(half):
            here = slice(head * DH, (head + 1) * DH)
            query, sums = query_ref[:, head_slice(start, head)], total_ref[:, here]
            for at, level_ref in zip(index, level_refs):
                reads = jnp.dot(query, level_ref[head], preferred_element_type=F32)
                sums = sums + reads * scale_ref[at, :, head : head + 1]
            square = jnp.mean(sums * sums, axis=-1, keepdims=True)
            normed_ref[:, here] = (sums * lax.rsqrt(square + 1e-06)).astype(BF16)

    arrays = [array for array, _ in levels]
    return local(kernel, [flip], [queries, scales, total, *arrays], [((rows, half * DH), BF16)])[0]


def project(mine, tokens, weights, jobs):
    rows, half = tokens[0][0].shape
    width = weights[0][0].shape[1]
    counts = [len(parts) for parts in weights]
    total_rows = rows * len(jobs)

    def kernel(mine_ref, *refs):
        token_refs, refs = refs[: 2 * len(tokens)], refs[2 * len(tokens) :]
        weight_refs = []
        for count in counts:
            weight_refs.append(refs[:count])
            refs = refs[count:]
        keep_ref, give_ref = refs
        ours = mine_ref[0] == 1

        def product(piece, part_refs):
            total, at = None, 0
            for part_ref in part_refs:
                end = at + part_ref.shape[0]
                for which in range(2):
                    low, high = max(at, which * half), min(end, (which + 1) * half)
                    if low < high:
                        one = jnp.dot(
                            token_refs[2 * piece + which][:, low - which * half : high - which * half],
                            part_ref[low - at : high - at, :],
                            preferred_element_type=F32,
                        )
                        total = one if total is None else total + one
                at = end
            return total

        for at, (piece, near, far) in enumerate(jobs):
            here = slice(at * rows, (at + 1) * rows)
            close, away = product(piece, weight_refs[near]), product(piece, weight_refs[far])
            keep_ref[here, :] = jnp.where(ours, close, away)
            give_ref[here, :] = jnp.where(ours, away, close).astype(BF16)

    shape = (total_rows, width)
    flat = [half_piece for pair in tokens for half_piece in pair] + [part for parts in weights for part in parts]
    return local(kernel, [mine], flat, [(shape, F32), (shape, BF16)])


def add_cores(keep, got, rows, groups):
    width = keep.shape[1]

    def kernel(keep_ref, got_ref, *out_refs):
        for group, out_ref in zip(groups, out_refs):
            for at, job in enumerate(group):
                here = slice(job * rows, (job + 1) * rows)
                total = keep_ref[here, :] + got_ref[here, :].astype(F32)
                out_ref[:, at * width : (at + 1) * width] = total.astype(BF16)

    return local(kernel, [], [keep, got], [((rows, width * len(group)), BF16) for group in groups])


def assemble(place, landed, width):
    rows = landed[0].shape[0]
    blocks = [piece.shape[1] // width for piece in landed]

    def copy_kernel(place_ref, *refs):
        out_ref, sems, at, copies = refs[-2], refs[-1], 0, []
        for ref, count in zip(refs, blocks):
            for block in range(count):
                column = pl.multiple_of(place_ref[at] * width, width)
                source = ref.at[:, block * width : (block + 1) * width]
                copies.append(pltpu.make_async_copy(source, out_ref.at[:, pl.ds(column, width)], sems.at[at]))
                copies[-1].start()
                at += 1
        for copy in copies:
            copy.wait()

    if width % 128:
        out, at = jnp.zeros((rows, width * sum(blocks)), BF16), 0
        for piece, count in zip(landed, blocks):
            for block in range(count):
                part = piece[:, block * width : (block + 1) * width]
                out = lax.dynamic_update_slice_in_dim(out, part, place[at] * width, 1)
                at += 1
        return out
    placed = [pltpu.with_memory_space_constraint(piece, pltpu.VMEM) for piece in landed]
    return pl.pallas_call(
        copy_kernel,
        out_shape=jax.ShapeDtypeStruct((rows, width * sum(blocks)), BF16),
        in_specs=[FLAT] + [HERE] * len(landed),
        out_specs=pl.BlockSpec(memory_space=pltpu.HBM),
        scratch_shapes=[pltpu.SemaphoreType.DMA((sum(blocks),))],
        compiler_params=SMALL,
        name="assemble",
    )(place, *placed)


def level_states(made, depth):
    top = depth - 1
    state, own = [part[0] for part in made], [part[1] for part in made]
    near, side, corner = [None, None], [None, None], [None, None]
    side[0] = swap(own[1], 2)
    near[0] = swap(own[0], 1)
    side[1] = swap(own[0], 2)
    corner[0] = swap(side[0], 1)
    near[1] = swap(own[1], 1)
    corner[1] = swap(near[0], 2)
    first, last = [], []
    for part in range(2):
        sent, block = block_sum(state[part], near[part], side[part], corner[part])
        early, late = [near[part], side[part], corner[part]], []
        for level in range(2, top - 1):
            other = swap(sent, 1 << level)
            early.append(other)
            sent, block = add_block(block, other, 1)
        level = top - 1
        if part == 0:
            other = lift(sent, 1 << level | 1 << top, 0, 1 << level)
            early.append(other)
            late.append((lift(sent, 1 << level, 1 << top, 1 << level), level + 1))
            (sent,) = add_block(block, other, 0)
            below = 1 << top - 1
            after = lift(sent, 1 << top, below, 1 << top)
            close = lift(sent, 1 << top, below, 1 << top | below)
            (got,) = add_block(after, close, 0)
            late.append((got, top + 1))
        else:
            late.append((lift(sent, 1 << level, 0, 1 << level), level + 1))
            late.append((swap(got, 2), top + 1))
        first.append(early)
        last.append(late)
    return first, last


def shards(queries, keys, values, level_index, level_table, out_weight):
    rows = queries.shape[0]
    heads_here = level_table.shape[0]
    half = heads_here // 2
    position = lax.axis_index("seq")
    core = lax.axis_index("head")
    depth = lax.axis_size("seq").bit_length() - 1
    top = depth - 1
    token_bits, column_bits = groups(depth)

    flip = position >> 1 & 1

    turn = jnp.full((1,), flip, jnp.int32)
    made = states(turn, keys, values, half)
    split = out_weight.shape[0] * 5 // 8
    parts = order_rows(turn, out_weight, split)
    far = swap(parts[0], 1 << top)
    down = lift(parts[1], 0, 1 << top, 1 << top)
    up = lift(parts[1], 1 << top, 0, 1 << top)
    weights_of = {0: parts, 1 << top: (far, down, up)}
    for bit in column_bits:
        for mask in list(weights_of):
            new, got = mask | 1 << bit, []
            for at, part in enumerate(weights_of[mask]):
                if at == 0 or not mask & 1 << top:
                    got.append(swap(part, 1 << bit))
                else:
                    got.append(swap_some(part, 1 << bit, 1 << top, at - 1))
            weights_of[new] = tuple(got)
    first, last = level_states(made, depth)

    inv_root = 1.0 / math.sqrt(DH)
    roots = [inv_root / math.sqrt(rows)] + [inv_root / math.sqrt(rows * 2**level) for level in range(depth)]
    flags = [None] + [level if level < top - 1 else None for level in range(depth)]
    spot = jnp.full((1,), position, jnp.int32)
    scales = level_scales(turn, spot, level_index, level_table, roots, flags, half)
    normed = []
    for part in range(2):
        total = first_reads(turn, queries, keys, values, scales[part], first[part], half, part)
        normed.append(last_reads(turn, queries, scales[part], total, last[part], half, part))

    pieces = {0: tuple(normed)}
    for mask in masks_of(token_bits)[1:]:
        bits = [bit for bit in token_bits if mask >> bit & 1]
        got = []
        for part in range(2):
            bit = bits[0] if part else bits[-1]
            source = 1 - part if bit == 1 else part
            got.append(swap(pieces[mask ^ 1 << bit][source], 1 << bit))
        pieces[mask] = tuple(got)
    token_masks = sorted(pieces)
    tokens = [pieces[mask] for mask in token_masks]
    mine = ((position >> top & 1) == core).astype(jnp.int32)[None]
    column_masks = masks_of(column_bits)
    staged = {mask: both if len(both) == 2 else (both[0], merge(both[1], both[2])) for mask, both in weights_of.items()}
    width, count, low = out_weight.shape[1], len(token_masks), (1 << top) - 1
    keep, give = project(mine, tokens[:-1], [staged[0], staged[1 << top]], [(at, 0, 1) for at in range(count - 1)])
    got = swap_cores(give)
    out, blocks = [], []
    sums = add_cores(keep, got, rows, [[at] for at in range(count - 1)])
    for mask, piece in zip(token_masks, sums):
        out.append(swap(piece, mask) if mask else piece)
        blocks.append(mask)
    jobs, groups_of = [], [[] for _ in range(count)]
    for at, mask in enumerate(column_masks):
        for piece in range(count):
            if at or piece == count - 1:
                groups_of[piece].append(len(jobs))
                jobs.append((piece, 2 * at, 2 * at + 1))
    weights = [staged[full] for mask in column_masks for full in (mask, mask | 1 << top)]
    keep, give = project(mine, tokens, weights, jobs)
    got = swap_cores(give)
    for piece, part in enumerate(add_cores(keep, got, rows, groups_of)):
        mask = token_masks[piece]
        out.append(swap(part, mask) if mask else part)
        blocks += [mask | column_mask for column_mask in column_masks[piece < count - 1 :]]
    place = jnp.stack([position & low ^ block for block in blocks]).astype(jnp.int32)
    return assemble(place, out, width)


def solution(mesh):
    placed = (
        P("seq", "head"),
        P("seq", "head"),
        P("seq", "head"),
        P("seq", None),
        P("head", None),
        P("head", "seq"),
    )
    return jax.shard_map(
        shards, mesh=mesh, in_specs=placed, out_specs=P("seq", "head"), check_vma=False
    )
```

```python
import math

import jax
import jax.numpy as jnp
from jax import lax
from jax.experimental import pallas as pl
from jax.experimental.pallas import tpu as pltpu
from jax.sharding import PartitionSpec as P

DH = 128


def swap(value, mask):
    pairs = [(source, source ^ mask) for source in range(lax.axis_size("seq"))]
    return lax.ppermute(value, "seq", pairs)


def lift(value, clear, need, mask):
    pairs = [
        (source, source ^ mask)
        for source in range(lax.axis_size("seq"))
        if not source & clear and source & need == need
    ]
    return lax.ppermute(value, "seq", pairs)


def swap_some(value, mask, half, upper):
    pairs = [
        (source, source ^ mask)
        for source in range(lax.axis_size("seq"))
        if (source & half != 0) == bool(upper)
    ]
    return lax.ppermute(value, "seq", pairs)


def swap_cores(value):
    return lax.ppermute(value, "head", [(0, 1), (1, 0)])


def masks_of(bits):
    out = [0]
    for bit in bits:
        out = out + [mask | 1 << bit for mask in out]
    return out


def groups(depth):
    top = depth - 1
    token_bits = [1, top - 1] if depth < 6 else [1, 2, top - 1]
    column_bits = [bit for bit in range(top) if bit not in token_bits][::-1]
    return token_bits, column_bits


HERE = pl.BlockSpec(memory_space=pltpu.VMEM)
FLAT = pl.BlockSpec(memory_space=pltpu.SMEM)
SMALL = pltpu.CompilerParams(vmem_limit_bytes=8 << 20)
F32, BF16 = jnp.float32, jnp.bfloat16


def local(kernel, scalars, operands, results, spare=()):
    placed = [pltpu.with_memory_space_constraint(operand, pltpu.VMEM) for operand in operands]
    return pl.pallas_call(
        kernel,
        out_shape=tuple(pltpu.VMEM(shape, dtype) for shape, dtype in results),
        in_specs=[FLAT] * len(scalars) + [HERE] * len(operands),
        out_specs=tuple(HERE for _ in results),
        scratch_shapes=[pltpu.VMEM(shape, BF16) for shape in spare],
        compiler_params=SMALL,
    )(*scalars, *placed)


def head_slice(start, head):
    return pl.ds(pl.multiple_of((start + head) * DH, DH), DH)


def states(flip, keys, values, half):
    rows, depth = keys.shape[0], half * DH

    def kernel(flip_ref, key_hbm, value_hbm, sum1_ref, own1_ref, sum0_ref, own0_ref, key_ref, value_ref, sems):
        copies = {}
        for part in (1, 0):
            start = pl.multiple_of(jnp.where(flip_ref[0] == part, 0, depth), depth)
            for at, (source, target) in enumerate(((key_hbm, key_ref), (value_hbm, value_ref))):
                copies[part, at] = pltpu.make_async_copy(
                    source.at[:, pl.ds(start, depth)], target.at[part], sems.at[part, at]
                )
                copies[part, at].start()
        for part, sum_ref, own_ref in ((1, sum1_ref, own1_ref), (0, sum0_ref, own0_ref)):
            copies[part, 0].wait()
            copies[part, 1].wait()
            for head in range(half):
                cut = slice(head * DH, (head + 1) * DH)
                state = lax.dot_general(
                    key_ref[part, :, cut],
                    value_ref[part, :, cut],
                    (((0,), (0,)), ((), ())),
                    preferred_element_type=F32,
                )
                sum_ref[head] = state
                own_ref[head] = state.astype(BF16)

    shape = (half, DH, DH)
    anywhere = pl.BlockSpec(memory_space=pltpu.HBM)
    made = pl.pallas_call(
        kernel,
        out_shape=(jax.ShapeDtypeStruct(shape, F32), pltpu.VMEM(shape, BF16)) * 2,
        in_specs=[FLAT, anywhere, anywhere],
        out_specs=(HERE,) * 4,
        scratch_shapes=[
            pltpu.VMEM((2, rows, depth), BF16),
            pltpu.VMEM((2, rows, depth), BF16),
            pltpu.SemaphoreType.DMA((2, 2)),
        ],
        compiler_params=SMALL,
        name="state",
    )(flip, *(pltpu.with_memory_space_constraint(operand, pltpu.HBM) for operand in (keys, values)))
    return [made[2:], made[:2]]


def order_rows(flip, weight, split):
    depth, width = weight.shape
    half = depth // 2
    sizes = (split, depth - split)

    def kernel(flip_ref, weight_ref, *refs):
        out_refs, sems = refs[:2], refs[2]
        copies = []
        for out, (low, size) in enumerate(((0, split), (split, depth - split))):
            for which in range(2):
                begin, end = max(low, which * half), min(low + size, (which + 1) * half)
                if begin < end:
                    start = pl.multiple_of(jnp.where(flip_ref[0] == which, 0, half), half)
                    copies.append(
                        pltpu.make_async_copy(
                            weight_ref.at[pl.ds(start + begin - which * half, end - begin)],
                            out_refs[out].at[pl.ds(begin - low, end - begin)],
                            sems.at[len(copies)],
                        )
                    )
        for copy in copies:
            copy.start()
        for copy in copies:
            copy.wait()

    return pl.pallas_call(
        kernel,
        out_shape=tuple(pltpu.VMEM((size, width), weight.dtype) for size in sizes),
        in_specs=[FLAT, pl.BlockSpec(memory_space=pltpu.HBM)],
        out_specs=(HERE, HERE),
        scratch_shapes=[pltpu.SemaphoreType.DMA((4,))],
        compiler_params=SMALL,
        name="order",
    )(flip, pltpu.with_memory_space_constraint(weight, pltpu.HBM))


def level_scales(flip, position, level_index, level_table, roots, flags, half):
    rows, values = level_index.shape[1], level_table.shape[1]

    def kernel(flip_ref, position_ref, index_ref, table_ref, *out_refs):
        for part, out_ref in enumerate(out_refs):
            start = pl.multiple_of(jnp.where(flip_ref[0] == part, 0, half), half)
            table = table_ref[pl.ds(start, half), :]
            for level, root in enumerate(roots):
                chosen = index_ref[level : level + 1, :] == lax.broadcasted_iota(
                    jnp.int32, (values, rows), 0
                )
                lam = lax.dot_general(
                    chosen.astype(F32),
                    table,
                    (((0,), (1,)), ((), ())),
                    precision=lax.Precision.HIGHEST,
                    preferred_element_type=F32,
                )
                scale = lam * root
                if flags[level] is not None:
                    scale = jnp.where(position_ref[0] >> flags[level] & 1 == 1, scale, 0.0)
                out_ref[level] = scale

    shape = (len(roots), rows, half)
    return local(kernel, [flip, position], [level_index, level_table], [(shape, F32), (shape, F32)])


def block_sum(state, near, side, corner):
    def kernel(state_ref, near_ref, side_ref, corner_ref, sent_ref, block_ref):
        for head in range(state.shape[0]):
            pair = side_ref[head].astype(F32) + corner_ref[head].astype(F32)
            block = state_ref[head] + near_ref[head].astype(F32) + pair
            sent_ref[head] = block.astype(BF16)
            block_ref[head] = block

    results = [(state.shape, BF16), (state.shape, F32)]
    return local(kernel, [], [state, near, side, corner], results)


def add_block(block, other, wide):
    def kernel(block_ref, other_ref, *out_refs):
        for head in range(block.shape[0]):
            total = block_ref[head].astype(F32) + other_ref[head].astype(F32)
            for out_ref in out_refs:
                out_ref[head] = total.astype(out_ref.dtype)

    results = [(block.shape, BF16)] + [(block.shape, F32)] * wide
    return local(kernel, [], [block, other], results)


def first_reads(flip, queries, keys, values, scales, levels, half, part):
    rows = queries.shape[0]

    def kernel(flip_ref, query_ref, key_ref, value_ref, scale_ref, *refs):
        level_refs, total_ref = refs[:-1], refs[-1]
        start = jnp.where(flip_ref[0] == part, 0, half)
        causal = lax.broadcasted_iota(jnp.int32, (rows, rows), 0) >= lax.broadcasted_iota(
            jnp.int32, (rows, rows), 1
        )
        for head in range(half):
            cut = head_slice(start, head)
            query = query_ref[:, cut]
            scores = lax.dot_general(
                query, key_ref[:, cut], (((1,), (1,)), ((), ())), preferred_element_type=F32
            )
            weights = jnp.where(causal, scores * scale_ref[0, :, head : head + 1], 0.0).astype(BF16)
            total = jnp.dot(weights, value_ref[:, cut], preferred_element_type=F32)
            pair = (level_refs[1][head].astype(F32) + level_refs[2][head].astype(F32)).astype(BF16)
            found = [level_refs[0][head], pair] + [level_ref[head] for level_ref in level_refs[3:]]
            for at, level in enumerate(found):
                reads = jnp.dot(query, level, preferred_element_type=F32)
                total = total + reads * scale_ref[at + 1, :, head : head + 1]
            total_ref[:, head * DH : (head + 1) * DH] = total

    return local(kernel, [flip], [queries, keys, values, scales, *levels], [((rows, half * DH), F32)])[0]


def last_reads(flip, queries, scales, total, levels, half, part):
    rows = queries.shape[0]
    index = [at for _, at in levels]

    def kernel(flip_ref, query_ref, scale_ref, total_ref, *refs):
        level_refs, normed_ref = refs[:-1], refs[-1]
        start = jnp.where(flip_ref[0] == part, 0, half)
        for head in range(half):
            here = slice(head * DH, (head + 1) * DH)
            query, sums = query_ref[:, head_slice(start, head)], total_ref[:, here]
            for at, level_ref in zip(index, level_refs):
                reads = jnp.dot(query, level_ref[head], preferred_element_type=F32)
                sums = sums + reads * scale_ref[at, :, head : head + 1]
            square = jnp.mean(sums * sums, axis=-1, keepdims=True)
            normed_ref[:, here] = (sums * lax.rsqrt(square + 1e-06)).astype(BF16)

    arrays = [array for array, _ in levels]
    return local(kernel, [flip], [queries, scales, total, *arrays], [((rows, half * DH), BF16)])[0]


def project(mine, tokens, weights, jobs):
    rows, half = tokens[0][0].shape
    width = weights[0][0].shape[1]
    counts = [len(parts) for parts in weights]
    merged = [parts[-1].shape for parts in weights if len(parts) == 3]
    shape = (rows * len(jobs), width)

    def kernel(mine_ref, *refs):
        token_refs, refs = refs[: 2 * len(tokens)], refs[2 * len(tokens) :]
        weight_refs = []
        for count in counts:
            weight_refs.append(refs[:count])
            refs = refs[count:]
        (keep_ref, give_ref), spare = refs[:2], list(refs[2:])
        for which, part_refs in enumerate(weight_refs):
            if len(part_refs) == 3:
                sum_ref = spare.pop(0)
                sum_ref[...] = part_refs[1][...] + part_refs[2][...]
                weight_refs[which] = (part_refs[0], sum_ref)
        ours = mine_ref[0] == 1

        def product(piece, part_refs):
            total, at = None, 0
            for part_ref in part_refs:
                end = at + part_ref.shape[0]
                for which in range(2):
                    low, high = max(at, which * half), min(end, (which + 1) * half)
                    if low < high:
                        one = jnp.dot(
                            token_refs[2 * piece + which][:, low - which * half : high - which * half],
                            part_ref[low - at : high - at, :],
                            preferred_element_type=F32,
                        )
                        total = one if total is None else total + one
                at = end
            return total

        for at, (piece, near, far) in enumerate(jobs):
            here = slice(at * rows, (at + 1) * rows)
            close, away = product(piece, weight_refs[near]), product(piece, weight_refs[far])
            keep_ref[here, :] = jnp.where(ours, close, away)
            give_ref[here, :] = jnp.where(ours, away, close).astype(BF16)

    flat = [part for pair in tokens for part in pair] + [part for parts in weights for part in parts]
    return local(kernel, [mine], flat, [(shape, F32), (shape, BF16)], merged)


def add_cores(keep, got, rows, groups):
    width = keep.shape[1]

    def kernel(keep_ref, got_ref, *out_refs):
        for group, out_ref in zip(groups, out_refs):
            for at, job in enumerate(group):
                here = slice(job * rows, (job + 1) * rows)
                total = keep_ref[here, :] + got_ref[here, :].astype(F32)
                out_ref[:, at * width : (at + 1) * width] = total.astype(BF16)

    return local(kernel, [], [keep, got], [((rows, width * len(group)), BF16) for group in groups])


def assemble(place, landed, width):
    rows = landed[0].shape[0]
    blocks = [piece.shape[1] // width for piece in landed]

    def copy_kernel(place_ref, *refs):
        out_ref, sems, at, copies = refs[-2], refs[-1], 0, []
        for ref, count in zip(refs, blocks):
            for block in range(count):
                column = pl.multiple_of(place_ref[at] * width, width)
                source = ref.at[:, block * width : (block + 1) * width]
                copies.append(pltpu.make_async_copy(source, out_ref.at[:, pl.ds(column, width)], sems.at[at]))
                copies[-1].start()
                at += 1
        for copy in copies:
            copy.wait()

    if width % 128:
        out, at = jnp.zeros((rows, width * sum(blocks)), BF16), 0
        for piece, count in zip(landed, blocks):
            for block in range(count):
                part = piece[:, block * width : (block + 1) * width]
                out = lax.dynamic_update_slice_in_dim(out, part, place[at] * width, 1)
                at += 1
        return out
    return pl.pallas_call(
        copy_kernel,
        out_shape=jax.ShapeDtypeStruct((rows, width * sum(blocks)), BF16),
        in_specs=[FLAT] + [pl.BlockSpec(memory_space=pl.ANY)] * len(landed),
        out_specs=pl.BlockSpec(memory_space=pltpu.HBM),
        scratch_shapes=[pltpu.SemaphoreType.DMA((sum(blocks),))],
        compiler_params=SMALL,
        name="assemble",
    )(place, *landed)


def level_states(made, depth):
    top = depth - 1
    state, own = [part[0] for part in made], [part[1] for part in made]
    near, side, corner = [None, None], [None, None], [None, None]
    side[0] = swap(own[1], 2)
    near[0] = swap(own[0], 1)
    side[1] = swap(own[0], 2)
    corner[0] = swap(side[0], 1)
    near[1] = swap(own[1], 1)
    corner[1] = swap(near[0], 2)
    first, last = [], []
    for part in range(2):
        sent, block = block_sum(state[part], near[part], side[part], corner[part])
        early, late = [near[part], side[part], corner[part]], []
        for level in range(2, top - 1):
            other = swap(sent, 1 << level)
            early.append(other)
            sent, block = add_block(block, other, 1)
        level = top - 1
        if part == 0:
            other = lift(sent, 1 << level | 1 << top, 0, 1 << level)
            early.append(other)
            late.append((lift(sent, 1 << level, 1 << top, 1 << level), level + 1))
            (sent,) = add_block(block, other, 0)
            below = 1 << top - 1
            after = lift(sent, 1 << top, below, 1 << top)
            close = lift(sent, 1 << top, below, 1 << top | below)
            (got,) = add_block(after, close, 0)
            late.append((got, top + 1))
        else:
            late.append((lift(sent, 1 << level, 0, 1 << level), level + 1))
            late.append((swap(got, 2), top + 1))
        first.append(early)
        last.append(late)
    return first, last


def shards(queries, keys, values, level_index, level_table, out_weight):
    rows = queries.shape[0]
    heads_here = level_table.shape[0]
    half = heads_here // 2
    position = lax.axis_index("seq")
    core = lax.axis_index("head")
    depth = lax.axis_size("seq").bit_length() - 1
    top = depth - 1
    token_bits, column_bits = groups(depth)

    flip = position >> 1 & 1

    turn = jnp.full((1,), flip, jnp.int32)
    made = states(turn, keys, values, half)
    split = out_weight.shape[0] * 11 // 16
    parts = order_rows(turn, out_weight, split)
    far = swap(parts[0], 1 << top)
    down = lift(parts[1], 0, 1 << top, 1 << top)
    up = lift(parts[1], 1 << top, 0, 1 << top)
    weights_of = {0: parts, 1 << top: (far, down, up)}
    for bit in column_bits:
        for mask in list(weights_of):
            new, got = mask | 1 << bit, []
            for at, part in enumerate(weights_of[mask]):
                if at == 0 or not mask & 1 << top:
                    got.append(swap(part, 1 << bit))
                else:
                    got.append(swap_some(part, 1 << bit, 1 << top, at - 1))
            weights_of[new] = tuple(got)
    first, last = level_states(made, depth)

    inv_root = 1.0 / math.sqrt(DH)
    roots = [inv_root / math.sqrt(rows)] + [inv_root / math.sqrt(rows * 2**level) for level in range(depth)]
    flags = [None] + [level if level < top - 1 else None for level in range(depth)]
    spot = jnp.full((1,), position, jnp.int32)
    scales = level_scales(turn, spot, level_index.T, level_table, roots, flags, half)
    normed = []
    for part in range(2):
        total = first_reads(turn, queries, keys, values, scales[part], first[part], half, part)
        normed.append(last_reads(turn, queries, scales[part], total, last[part], half, part))

    pieces = {0: tuple(normed)}
    for mask in masks_of(token_bits)[1:]:
        bits = [bit for bit in token_bits if mask >> bit & 1]
        got = []
        for part in range(2):
            bit = bits[0] if part else bits[-1]
            source = 1 - part if bit == 1 else part
            got.append(swap(pieces[mask ^ 1 << bit][source], 1 << bit))
        pieces[mask] = tuple(got)
    token_masks = sorted(pieces)
    tokens = [pieces[mask] for mask in token_masks]
    mine = ((position >> top & 1) == core).astype(jnp.int32)[None]
    column_masks = masks_of(column_bits)
    width, count, low = out_weight.shape[1], len(token_masks), (1 << top) - 1
    out, blocks = [], []

    def leave(keep, give, groups_of, covers):
        got = swap_cores(give)
        chosen = [piece for piece in range(len(groups_of)) if groups_of[piece]]
        sums = add_cores(keep, got, rows, [groups_of[piece] for piece in chosen])
        for piece, part in zip(chosen, sums):
            mask = token_masks[piece]
            out.append(swap(part, mask) if mask else part)
            blocks.extend(mask | cover for cover in covers[piece])

    early = [(at, 0, 1) for at in range(count - 1)]
    keep, give = project(mine, tokens[:-1], [weights_of[0], weights_of[1 << top]], early)
    leave(keep, give, [[at] for at in range(count - 1)], [[0]] * (count - 1))
    jobs, groups_of, covers = [], [[] for _ in range(count)], [[] for _ in range(count)]
    for at, mask in enumerate(column_masks):
        for piece in range(count):
            if at or piece == count - 1:
                groups_of[piece].append(len(jobs))
                covers[piece].append(mask)
                jobs.append((piece, 2 * at, 2 * at + 1))
    weights = [weights_of[full] for mask in column_masks for full in (mask, mask | 1 << top)]
    keep, give = project(mine, tokens, weights, jobs)
    leave(keep, give, groups_of, covers)
    place = jnp.stack([position & low ^ block for block in blocks]).astype(jnp.int32)
    return assemble(place, out, width)


def solution(mesh):
    placed = (
        P("seq", "head"),
        P("seq", "head"),
        P("seq", "head"),
        P("seq", None),
        P("head", None),
        P("head", "seq"),
    )
    return jax.shard_map(
        shards, mesh=mesh, in_specs=placed, out_specs=P("seq", "head"), check_vma=False
    )
```

```python
import math

import jax
import jax.numpy as jnp
from jax import lax
from jax.experimental import pallas as pl
from jax.experimental.pallas import tpu as pltpu
from jax.sharding import PartitionSpec as P

DH = 128


def swap(value, mask):
    pairs = [(source, source ^ mask) for source in range(lax.axis_size("seq"))]
    return lax.ppermute(value, "seq", pairs)


def lift(value, clear, need, mask):
    pairs = [
        (source, source ^ mask)
        for source in range(lax.axis_size("seq"))
        if not source & clear and source & need == need
    ]
    return lax.ppermute(value, "seq", pairs)


def swap_some(value, mask, half, upper):
    pairs = [
        (source, source ^ mask)
        for source in range(lax.axis_size("seq"))
        if (source & half != 0) == bool(upper)
    ]
    return lax.ppermute(value, "seq", pairs)


def swap_at(value, mask, bits, want):
    pairs = [(source, source ^ mask) for source in range(lax.axis_size("seq")) if source & bits == want]
    return lax.ppermute(value, "seq", pairs)


def swap_cores(value):
    return lax.ppermute(value, "head", [(0, 1), (1, 0)])


def masks_of(bits):
    out = [0]
    for bit in bits:
        out = out + [mask | 1 << bit for mask in out]
    return out


def groups(depth):
    top = depth - 1
    token_bits = [1, top - 1] if depth < 6 else [1, 2, top - 1]
    column_bits = [bit for bit in range(top) if bit not in token_bits][::-1]
    return token_bits, column_bits


HERE = pl.BlockSpec(memory_space=pltpu.VMEM)
FLAT = pl.BlockSpec(memory_space=pltpu.SMEM)
SMALL = pltpu.CompilerParams(vmem_limit_bytes=8 << 20)
F32, BF16 = jnp.float32, jnp.bfloat16


def local(kernel, scalars, operands, results, spare=(), params=SMALL):
    placed = [pltpu.with_memory_space_constraint(operand, pltpu.VMEM) for operand in operands]
    return pl.pallas_call(
        kernel,
        out_shape=tuple(pltpu.VMEM(shape, dtype) for shape, dtype in results),
        in_specs=[FLAT] * len(scalars) + [HERE] * len(operands),
        out_specs=tuple(HERE for _ in results),
        scratch_shapes=[pltpu.VMEM(shape, BF16) for shape in spare],
        compiler_params=params,
    )(*scalars, *placed)


def head_slice(start, head):
    return pl.ds(pl.multiple_of((start + head) * DH, DH), DH)


def states(flip, keys, values, half):
    rows, depth = keys.shape[0], half * DH

    def kernel(flip_ref, key_hbm, value_hbm, sum1_ref, own1_ref, sum0_ref, own0_ref, key_ref, value_ref, sems):
        copies = {}
        for part in (1, 0):
            start = pl.multiple_of(jnp.where(flip_ref[0] == part, 0, depth), depth)
            for at, (source, target) in enumerate(((key_hbm, key_ref), (value_hbm, value_ref))):
                copies[part, at] = pltpu.make_async_copy(
                    source.at[:, pl.ds(start, depth)], target.at[part], sems.at[part, at]
                )
                copies[part, at].start()
        for part, sum_ref, own_ref in ((1, sum1_ref, own1_ref), (0, sum0_ref, own0_ref)):
            copies[part, 0].wait()
            copies[part, 1].wait()
            for head in range(half):
                cut = slice(head * DH, (head + 1) * DH)
                state = lax.dot_general(
                    key_ref[part, :, cut],
                    value_ref[part, :, cut],
                    (((0,), (0,)), ((), ())),
                    preferred_element_type=F32,
                )
                sum_ref[head] = state
                own_ref[head] = state.astype(BF16)

    shape = (half, DH, DH)
    anywhere = pl.BlockSpec(memory_space=pltpu.HBM)
    made = pl.pallas_call(
        kernel,
        out_shape=(jax.ShapeDtypeStruct(shape, F32), pltpu.VMEM(shape, BF16)) * 2,
        in_specs=[FLAT, anywhere, anywhere],
        out_specs=(HERE,) * 4,
        scratch_shapes=[
            pltpu.VMEM((2, rows, depth), BF16),
            pltpu.VMEM((2, rows, depth), BF16),
            pltpu.SemaphoreType.DMA((2, 2)),
        ],
        compiler_params=SMALL,
        name="state",
    )(flip, *(pltpu.with_memory_space_constraint(operand, pltpu.HBM) for operand in (keys, values)))
    return [made[2:], made[:2]]


def order_rows(flip, weight, split):
    depth, width = weight.shape
    half = depth // 2
    sizes = (split, depth - split)

    def kernel(flip_ref, weight_ref, *refs):
        out_refs, sems = refs[:2], refs[2]
        copies = []
        for out, (low, size) in enumerate(((0, split), (split, depth - split))):
            for which in range(2):
                begin, end = max(low, which * half), min(low + size, (which + 1) * half)
                if begin < end:
                    start = pl.multiple_of(jnp.where(flip_ref[0] == which, 0, half), half)
                    copies.append(
                        pltpu.make_async_copy(
                            weight_ref.at[pl.ds(start + begin - which * half, end - begin)],
                            out_refs[out].at[pl.ds(begin - low, end - begin)],
                            sems.at[len(copies)],
                        )
                    )
        for copy in copies:
            copy.start()
        for copy in copies:
            copy.wait()

    return pl.pallas_call(
        kernel,
        out_shape=tuple(pltpu.VMEM((size, width), weight.dtype) for size in sizes),
        in_specs=[FLAT, pl.BlockSpec(memory_space=pltpu.HBM)],
        out_specs=(HERE, HERE),
        scratch_shapes=[pltpu.SemaphoreType.DMA((4,))],
        compiler_params=SMALL,
        name="order",
    )(flip, pltpu.with_memory_space_constraint(weight, pltpu.HBM))


def level_scales(flip, position, level_index, level_table, roots, flags, half):
    rows, values = level_index.shape[1], level_table.shape[1]

    def kernel(flip_ref, position_ref, index_ref, table_ref, *out_refs):
        for part, out_ref in enumerate(out_refs):
            start = pl.multiple_of(jnp.where(flip_ref[0] == part, 0, half), half)
            table = table_ref[pl.ds(start, half), :]
            for level, root in enumerate(roots):
                chosen = index_ref[level : level + 1, :] == lax.broadcasted_iota(
                    jnp.int32, (values, rows), 0
                )
                lam = lax.dot_general(
                    chosen.astype(F32),
                    table,
                    (((0,), (1,)), ((), ())),
                    precision=lax.Precision.HIGHEST,
                    preferred_element_type=F32,
                )
                scale = lam * root
                if flags[level] is not None:
                    scale = jnp.where(position_ref[0] >> flags[level] & 1 == 1, scale, 0.0)
                out_ref[level] = scale

    shape = (len(roots), rows, half)
    return local(kernel, [flip, position], [level_index, level_table], [(shape, F32), (shape, F32)])


def block_sum(state, near, side, corner):
    def kernel(state_ref, near_ref, side_ref, corner_ref, sent_ref, block_ref):
        for head in range(state.shape[0]):
            pair = side_ref[head].astype(F32) + corner_ref[head].astype(F32)
            block = state_ref[head] + near_ref[head].astype(F32) + pair
            sent_ref[head] = block.astype(BF16)
            block_ref[head] = block

    results = [(state.shape, BF16), (state.shape, F32)]
    return local(kernel, [], [state, near, side, corner], results)


def add_block(block, other, wide):
    def kernel(block_ref, other_ref, *out_refs):
        for head in range(block.shape[0]):
            total = block_ref[head].astype(F32) + other_ref[head].astype(F32)
            for out_ref in out_refs:
                out_ref[head] = total.astype(out_ref.dtype)

    results = [(block.shape, BF16)] + [(block.shape, F32)] * wide
    return local(kernel, [], [block, other], results)


def first_reads(flip, queries, keys, values, scales, levels, half, part):
    rows = queries.shape[0]

    def kernel(flip_ref, query_ref, key_ref, value_ref, scale_ref, *refs):
        level_refs, total_ref = refs[:-1], refs[-1]
        start = jnp.where(flip_ref[0] == part, 0, half)
        causal = lax.broadcasted_iota(jnp.int32, (rows, rows), 0) >= lax.broadcasted_iota(
            jnp.int32, (rows, rows), 1
        )
        for head in range(half):
            cut = head_slice(start, head)
            query = query_ref[:, cut]
            scores = lax.dot_general(
                query, key_ref[:, cut], (((1,), (1,)), ((), ())), preferred_element_type=F32
            )
            weights = jnp.where(causal, scores * scale_ref[0, :, head : head + 1], 0.0).astype(BF16)
            total = jnp.dot(weights, value_ref[:, cut], preferred_element_type=F32)
            pair = (level_refs[1][head].astype(F32) + level_refs[2][head].astype(F32)).astype(BF16)
            found = [level_refs[0][head], pair] + [level_ref[head] for level_ref in level_refs[3:]]
            for at, level in enumerate(found):
                reads = jnp.dot(query, level, preferred_element_type=F32)
                total = total + reads * scale_ref[at + 1, :, head : head + 1]
            total_ref[:, head * DH : (head + 1) * DH] = total

    return local(kernel, [flip], [queries, keys, values, scales, *levels], [((rows, half * DH), F32)])[0]


def last_reads(flip, queries, scales, total, levels, half, part):
    rows = queries.shape[0]
    index = [at for _, at in levels]

    def kernel(flip_ref, query_ref, scale_ref, total_ref, *refs):
        level_refs, normed_ref = refs[:-1], refs[-1]
        start = jnp.where(flip_ref[0] == part, 0, half)
        for head in range(half):
            here = slice(head * DH, (head + 1) * DH)
            query, sums = query_ref[:, head_slice(start, head)], total_ref[:, here]
            for at, level_ref in zip(index, level_refs):
                reads = jnp.dot(query, level_ref[head], preferred_element_type=F32)
                sums = sums + reads * scale_ref[at, :, head : head + 1]
            square = jnp.mean(sums * sums, axis=-1, keepdims=True)
            normed_ref[:, here] = (sums * lax.rsqrt(square + 1e-06)).astype(BF16)

    arrays = [array for array, _ in levels]
    return local(kernel, [flip], [queries, scales, total, *arrays], [((rows, half * DH), BF16)])[0]


def project(mine, tokens, weights, jobs):
    rows, half = tokens[0][0].shape
    width = weights[0][0].shape[1]
    counts = [len(parts) for parts in weights]
    merged = [parts[-1].shape for parts in weights if len(parts) == 3]
    shape = (rows * len(jobs), width)

    def kernel(mine_ref, *refs):
        token_refs, refs = refs[: 2 * len(tokens)], refs[2 * len(tokens) :]
        weight_refs = []
        for count in counts:
            weight_refs.append(refs[:count])
            refs = refs[count:]
        (keep_ref, give_ref), spare = refs[:2], list(refs[2:])
        for which, part_refs in enumerate(weight_refs):
            if len(part_refs) == 3:
                sum_ref = spare.pop(0)
                sum_ref[...] = part_refs[1][...] + part_refs[2][...]
                weight_refs[which] = (part_refs[0], sum_ref)
        ours = mine_ref[0] == 1

        def product(piece, part_refs):
            total, at = None, 0
            for part_ref in part_refs:
                end = at + part_ref.shape[0]
                for which in range(2):
                    low, high = max(at, which * half), min(end, (which + 1) * half)
                    if low < high:
                        one = jnp.dot(
                            token_refs[2 * piece + which][:, low - which * half : high - which * half],
                            part_ref[low - at : high - at, :],
                            preferred_element_type=F32,
                        )
                        total = one if total is None else total + one
                at = end
            return total

        for at, (piece, near, far) in enumerate(jobs):
            here = slice(at * rows, (at + 1) * rows)
            close, away = product(piece, weight_refs[near]), product(piece, weight_refs[far])
            keep_ref[here, :] = jnp.where(ours, close, away)
            give_ref[here, :] = jnp.where(ours, away, close).astype(BF16)

    flat = [part for pair in tokens for part in pair] + [part for parts in weights for part in parts]
    params = SMALL if len(jobs) <= 16 else pltpu.CompilerParams(vmem_limit_bytes=20 << 20)
    return local(kernel, [mine], flat, [(shape, F32), (shape, BF16)], merged, params)


def add_cores(keep, got, rows, groups):
    width = keep.shape[1]

    def kernel(keep_ref, got_ref, *out_refs):
        for group, out_ref in zip(groups, out_refs):
            for at, job in enumerate(group):
                here = slice(job * rows, (job + 1) * rows)
                total = keep_ref[here, :] + got_ref[here, :].astype(F32)
                out_ref[:, at * width : (at + 1) * width] = total.astype(BF16)

    return local(kernel, [], [keep, got], [((rows, width * len(group)), BF16) for group in groups])


def assemble(place, landed, width):
    rows = landed[0].shape[0]
    blocks = [piece.shape[1] // width for piece in landed]

    def copy_kernel(place_ref, *refs):
        out_ref, sems, at, copies = refs[-2], refs[-1], 0, []
        for ref, count in zip(refs, blocks):
            for block in range(count):
                column = pl.multiple_of(place_ref[at] * width, width)
                source = ref.at[:, block * width : (block + 1) * width]
                copies.append(pltpu.make_async_copy(source, out_ref.at[:, pl.ds(column, width)], sems.at[at]))
                copies[-1].start()
                at += 1
        for copy in copies:
            copy.wait()

    if width % 128:
        out, at = jnp.zeros((rows, width * sum(blocks)), BF16), 0
        for piece, count in zip(landed, blocks):
            for block in range(count):
                part = piece[:, block * width : (block + 1) * width]
                out = lax.dynamic_update_slice_in_dim(out, part, place[at] * width, 1)
                at += 1
        return out
    return pl.pallas_call(
        copy_kernel,
        out_shape=jax.ShapeDtypeStruct((rows, width * sum(blocks)), BF16),
        in_specs=[FLAT] + [pl.BlockSpec(memory_space=pl.ANY)] * len(landed),
        out_specs=pl.BlockSpec(memory_space=pltpu.HBM),
        scratch_shapes=[pltpu.SemaphoreType.DMA((sum(blocks),))],
        compiler_params=SMALL,
        name="assemble",
    )(place, *landed)


def level_states(made, depth):
    top = depth - 1
    state, own = [part[0] for part in made], [part[1] for part in made]
    near, side, corner = [None, None], [None, None], [None, None]
    side[0] = swap(own[1], 2)
    near[0] = swap(own[0], 1)
    side[1] = swap(own[0], 2)
    corner[0] = swap(side[0], 1)
    near[1] = swap(own[1], 1)
    corner[1] = swap(near[0], 2)
    first, last = [], []
    level, below = top - 1, 1 << top - 1
    for part in range(2):
        early, late = [near[part], side[part], corner[part]], []
        if part == 0 or level > 2:
            sent, block = block_sum(state[part], near[part], side[part], corner[part])
        for middle in range(2, level):
            other = swap(sent, 1 << middle)
            early.append(other)
            sent, block = add_block(block, other, 1)
        if part == 0:
            lower = lift(sent, below | 1 << top, 0, below)
            upper = lift(sent, below, 1 << top, below)
            early.append(lower)
            late.append((upper, level + 1))
            (sent,) = add_block(block, lower, 0)
            after = lift(sent, 1 << top, below, 1 << top)
            close = lift(sent, 1 << top, below, 1 << top | below)
            (got,) = add_block(after, close, 0)
            late.append((got, top + 1))
        else:
            both = below | 1 << top
            early.append(swap_at(lower, 2, both, below))
            late.append((swap_at(upper, 2, both, both), level + 1))
            late.append((swap(got, 2), top + 1))
        first.append(early)
        last.append(late)
    return first, last


def shards(queries, keys, values, level_index, level_table, out_weight):
    rows = queries.shape[0]
    heads_here = level_table.shape[0]
    half = heads_here // 2
    position = lax.axis_index("seq")
    core = lax.axis_index("head")
    depth = lax.axis_size("seq").bit_length() - 1
    top = depth - 1
    token_bits, column_bits = groups(depth)

    flip = position >> 1 & 1

    turn = jnp.full((1,), flip, jnp.int32)
    made = states(turn, keys, values, half)
    split = out_weight.shape[0] * 5 // 8
    parts = order_rows(turn, out_weight, split)
    far = swap(parts[0], 1 << top)
    down = lift(parts[1], 0, 1 << top, 1 << top)
    up = lift(parts[1], 1 << top, 0, 1 << top)
    weights_of = {0: parts, 1 << top: (far, down, up)}
    for bit in column_bits:
        for mask in list(weights_of):
            new, got = mask | 1 << bit, []
            for at, part in enumerate(weights_of[mask]):
                if at == 0 or not mask & 1 << top:
                    got.append(swap(part, 1 << bit))
                else:
                    got.append(swap_some(part, 1 << bit, 1 << top, at - 1))
            weights_of[new] = tuple(got)
    first, last = level_states(made, depth)

    inv_root = 1.0 / math.sqrt(DH)
    roots = [inv_root / math.sqrt(rows)] + [inv_root / math.sqrt(rows * 2**level) for level in range(depth)]
    flags = [None] + [level if level < top - 1 else None for level in range(depth)]
    spot = jnp.full((1,), position, jnp.int32)
    scales = level_scales(turn, spot, level_index.T, level_table, roots, flags, half)
    normed = []
    for part in range(2):
        total = first_reads(turn, queries, keys, values, scales[part], first[part], half, part)
        normed.append(last_reads(turn, queries, scales[part], total, last[part], half, part))

    pieces = {0: tuple(normed)}
    for mask in masks_of(token_bits)[1:]:
        bits = [bit for bit in token_bits if mask >> bit & 1]
        got = []
        for part in range(2):
            bit = bits[0] if part else bits[-1]
            source = 1 - part if bit == 1 else part
            got.append(swap(pieces[mask ^ 1 << bit][source], 1 << bit))
        pieces[mask] = tuple(got)
    token_masks = sorted(pieces)
    tokens = [pieces[mask] for mask in token_masks]
    mine = ((position >> top & 1) == core).astype(jnp.int32)[None]
    column_masks = masks_of(column_bits)
    width, count, low = out_weight.shape[1], len(token_masks), (1 << top) - 1
    out, blocks = [], []

    def leave(keep, give, groups_of, covers):
        got = swap_cores(give)
        chosen = [piece for piece in range(len(groups_of)) if groups_of[piece]]
        sums = add_cores(keep, got, rows, [groups_of[piece] for piece in chosen])
        for piece, part in zip(chosen, sums):
            mask = token_masks[piece]
            out.append(swap(part, mask) if mask else part)
            blocks.extend(mask | cover for cover in covers[piece])

    early = [(at, 0, 1) for at in range(count - 1)]
    keep, give = project(mine, tokens[:-1], [weights_of[0], weights_of[1 << top]], early)
    leave(keep, give, [[at] for at in range(count - 1)], [[0]] * (count - 1))
    jobs, groups_of, covers = [], [[] for _ in range(count)], [[] for _ in range(count)]
    for at, mask in enumerate(column_masks):
        for piece in range(count):
            if at or piece == count - 1:
                groups_of[piece].append(len(jobs))
                covers[piece].append(mask)
                jobs.append((piece, 2 * at, 2 * at + 1))
    weights = [weights_of[full] for mask in column_masks for full in (mask, mask | 1 << top)]
    keep, give = project(mine, tokens, weights, jobs)
    leave(keep, give, groups_of, covers)
    place = jnp.stack([position & low ^ block for block in blocks]).astype(jnp.int32)
    return assemble(place, out, width)


def solution(mesh):
    placed = (
        P("seq", "head"),
        P("seq", "head"),
        P("seq", "head"),
        P("seq", None),
        P("head", None),
        P("head", "seq"),
    )
    return jax.shard_map(
        shards, mesh=mesh, in_specs=placed, out_specs=P("seq", "head"), check_vma=False
    )
```
